32 devices in a mesh: blk: 8 (over y, x, core), ab: 4 (over z).
Axes of the slice: x: 2, y: 2, z: 4, core: 2. Of those that a mesh axis runs over, the one named last changes fastest.
Arguments:
- amplitudes: bfloat16 [512, 11264], P('blk'), may hold values from -6 to 6
- integrals: bfloat16 [4096, 11264], P(('blk', 'ab')), may hold values from -0.0546875 to 0.0546875
- live_rows: int32 [8], replicated, may hold values from 1 to 64, 320 in all
- partner: int32 [512], replicated, may hold values from 0 to 511, as said below
Outputs:
- ladder: float32 [512, 4096], P(None, ('blk', 'ab'))
The draws below stay inside these ranges and needn't reach their ends.
Inputs may be any that keep to these rules, and one draw needn't show every extreme that they name: `live_rows`: lengths of the blocks; the largest equals 64. An involution without fixed points: partner[partner[r]] = r and partner[r] != r.
All inputs are finite; a program needn't handle non-finite values.
Results may differ from the reference program's by a relative error of at most 0.0003.
Values may be sent and summed in bfloat16 or wider, within the bound.
A program may use at most 128 MiB of HBM per device.

```python
import math
import jax
import jax.numpy as jnp
import numpy as np
from jax import lax

CD = 11264
IJ_DEV = 64
AB_DEV = 128
BLOCKS = 8
IJ = 512
AB = 4096
HALF = 256
DEVICES = 32


def draw_partner(key, part):
    order = jax.random.permutation(key, IJ).astype(jnp.int32)
    paired = order.reshape(-1, 2)[:, ::-1].reshape(-1)
    return jnp.zeros((IJ,), jnp.int32).at[order].set(paired)


def level_of(key, dims, cuts, low, largest):
    def one(position, shards_of):
        steps = jax.random.uniform(jax.random.fold_in(jax.random.fold_in(key, 6), position), (shards_of,), jnp.float32, low / len(cuts), largest / len(cuts))
        return jnp.repeat(jnp.exp(steps), dims[position] // shards_of).reshape((-1,) + (1,) * (len(dims) - position - 1))

    gain = one(*cuts[0])
    for cut in cuts[1:]:
        gain = gain * one(*cut)
    return gain


def profile(count, total, limit, skew):
    loads = [(1 << 20) // math.isqrt(grade ** skew) + 1 for grade in range(2, count + 1)]
    spare, counts = total - limit - (count - 1), [1] * (count - 1)
    while spare > 0:
        free = [i for i in range(count - 1) if counts[i] < limit]
        mass, remaining = sum([loads[i] for i in free]), spare
        for i in free:
            extra = min(limit - counts[i], max(1, remaining * loads[i] // mass), spare)
            counts[i] = counts[i] + extra
            spare = spare - extra
    return np.array([limit] + counts)


def uneven(own_key, amount, total, limit, skew):
    if amount == 2:
        one = jax.random.randint(own_key, (), max(1, total - limit), min(limit, total - 1) + 1)
        return jnp.stack([one, total - one])
    lengths = jnp.asarray(profile(amount, total, limit, skew), jnp.int32)
    twos = (amount - 1) // 2
    source_of, sink = lengths[1:1 + 2 * twos:2], lengths[2:2 + 2 * twos:2]
    slack = jnp.minimum(source_of - 1, limit - sink)
    moved = jax.random.randint(jax.random.fold_in(own_key, 1), (twos,), 0, 1 << 20) % (slack + 1)
    lengths = lengths.at[1:1 + 2 * twos:2].set(source_of - moved).at[2:2 + 2 * twos:2].set(sink + moved)
    return lengths[jax.random.permutation(jax.random.fold_in(own_key, 2), amount)]


def noise(key, shape, width, most, pieces=(), held_as=jnp.bfloat16):
    drawn = width * jax.random.normal(key, shape, jnp.float32)
    if pieces:
        drawn = drawn * level_of(key, shape, pieces, -0.22, 0.18)
    return jnp.clip(drawn, -most, most).astype(held_as)


def setup_inputs(seed: int = 0) -> dict:
    key_list = jax.random.split(jax.random.key(seed), 5)
    return {
        "amplitudes": noise(key_list[0], (IJ, CD), 1.0, 6.0, ((0, 8),)),
        "integrals": noise(key_list[1], (AB, CD), CD ** -0.5, 0.0546875, ((0, 32),)),
        "live_rows": uneven(key_list[2], BLOCKS, IJ_DEV * BLOCKS * 5 // 8, IJ_DEV, 2).astype(jnp.int32),
        "partner": draw_partner(jax.random.fold_in(key_list[4], 71), 0),
    }


def reference(amplitudes, integrals, live_rows, partner):
    slots = jnp.arange(IJ, dtype=jnp.int32)
    live = (slots % IJ_DEV) < jnp.repeat(live_rows, IJ_DEV, total_repeat_length=IJ)
    blocks = integrals.reshape(DEVICES, AB_DEV, CD)

    def one_block(rows):
        return lax.dot_general(amplitudes, rows, (((1,), (1,)), ((), ())), preferred_element_type=jnp.float32)

    partial_w = lax.map(one_block, blocks)
    partial_w = jnp.transpose(partial_w, (1, 0, 2)).reshape(IJ, AB)
    partial_w = jnp.where(live[:, None], partial_w, jnp.zeros_like(partial_w))
    mated = partial_w.reshape(IJ, AB // (2 * HALF), 2, HALF)[:, :, ::-1, :].reshape(IJ, AB)
    return partial_w + mated[partner.astype(jnp.int32)]
```

```python
import functools

import jax
import jax.numpy as jnp
from jax import lax
from jax.experimental import pallas as pl
from jax.experimental.pallas import tpu as pltpu
from jax.sharding import PartitionSpec as P

CUBE = 8
QUARTERS = 4
PIECES = 4
LAG_RELAY = 1
LAG_DOT = 2

OWN, FIRST, SECOND, ACROSS = 0, 1, 2, 3
SOURCE = {1: 0, 4: 0, 2: 1, 3: 1, 5: 1, 6: 2, 7: 3}


def kernel(
    height, depth, live_ref, partner_ref, a_ref, b_ref, out_ref,
    held, integrals, tile, mated,
    send_sem, recv_sem, own_sem, b_sem, mate_send, mate_recv,
):
    blk, ab = lax.axis_index("blk"), lax.axis_index("ab")
    ab_size = lax.axis_size("ab")
    b = lax.rem(blk, CUBE)
    base = blk - b
    core, x, y = lax.rem(b, 2), lax.rem(lax.div(b, 2), 2), lax.rem(lax.div(b, 4), 2)
    parity = lax.rem(ab, 2)
    flip = 1 - 2 * core
    near_x, near_y = b + 2 - 4 * x, b + 4 - 8 * y
    first = near_x + parity * (near_y - near_x)
    other = near_x + near_y - first
    diagonal = near_x + near_y - b
    blocks = [b, first, diagonal, other]
    blocks = blocks + [i + flip for i in blocks]
    to_first = (base + first, ab)
    to_second = (base + other, ab)
    to_across = (blk, ab + 1 - 2 * parity)
    to_sibling = (blk + flip, ab)
    to_mate = (blk, lax.rem(ab + ab_size // 2, ab_size))
    target = {1: to_first, 2: to_second, 3: to_across}
    target.update({slot: to_sibling for slot in (4, 5, 6, 7)})

    rows = a_ref.shape[0] // QUARTERS
    steps = QUARTERS * PIECES

    def where(t):
        return t // PIECES, pl.ds((t % PIECES) * depth, depth)

    def remote(slot, t):
        q, columns = where(t)
        if SOURCE[slot] == OWN:
            src = a_ref.at[pl.ds(q * rows, rows), columns]
        else:
            src = held.at[q, SOURCE[slot], :, columns]
        return pltpu.make_async_remote_copy(
            src_ref=src,
            dst_ref=held.at[q, slot, :, columns],
            send_sem=send_sem.at[slot, t],
            recv_sem=recv_sem.at[slot, t],
            device_id=target[slot],
            device_id_type=pl.DeviceIdType.MESH,
        )

    def mate(q):
        band = pl.ds(q * rows, rows)
        return pltpu.make_async_remote_copy(
            src_ref=tile.at[:, band, :],
            dst_ref=mated.at[:, band, :],
            send_sem=mate_send.at[q],
            recv_sem=mate_recv.at[q],
            device_id=to_mate,
            device_id_type=pl.DeviceIdType.MESH,
        )

    def load_b(k):
        columns = pl.ds(k * depth, depth)
        return pltpu.make_async_copy(b_ref.at[:, columns], integrals.at[:, columns], b_sem.at[k])

    def load_own(q):
        return pltpu.make_async_copy(a_ref.at[pl.ds(q * rows, rows), :], held.at[q, OWN], own_sem.at[q])

    barrier = pltpu.get_barrier_semaphore()
    neighbours = (to_first, to_second, to_across, to_sibling, to_mate)
    for device in neighbours:
        pl.semaphore_signal(barrier, inc=1, device_id=device, device_id_type=pl.DeviceIdType.MESH)
    pl.semaphore_wait(barrier, len(neighbours))

    for t in range(steps):
        remote(1, t).start()
        remote(4, t).start()
    for k in range(PIECES):
        load_b(k).start()
    for q in range(QUARTERS):
        load_own(q).start()

    total = None
    for step in range(steps + LAG_DOT):
        if step < steps:
            remote(1, step).wait_recv()
            for slot in (2, 3, 5):
                remote(slot, step).start()
        t = step - LAG_RELAY
        if 0 <= t < steps:
            remote(2, t).wait_recv()
            remote(6, t).start()
            remote(3, t).wait_recv()
            remote(7, t).start()
        t = step - LAG_DOT
        if t >= 0:
            q, columns = where(t)
            k = t % PIECES
            if k == 0:
                load_own(q).wait()
            if q == 0:
                load_b(k).wait()
            for slot in (4, 5, 6, 7):
                remote(slot, t).wait_recv()
            left = held[q, :, :, columns].reshape(CUBE * rows, depth)
            product = lax.dot_general(
                left, integrals[:, columns], (((1,), (1,)), ((), ())),
                preferred_element_type=jnp.float32,
            )
            total = product if k == 0 else total + product
            if k == PIECES - 1:
                group, inside = (q * rows) // height, (q * rows) % height
                repeats = a_ref.shape[0] // height
                row = inside + lax.broadcasted_iota(jnp.int32, (rows, total.shape[1]), 0)
                for slot in range(CUBE):
                    part = total[slot * rows:(slot + 1) * rows]
                    limit = live_ref[blocks[slot] * repeats + group]
                    tile[blocks[slot], pl.ds(q * rows, rows), :] = jnp.where(row < limit, part, 0.0)
                mate(q).start()

    for q in range(QUARTERS):
        mate(q).wait_recv()
    span = a_ref.shape[0]
    for i in range(CUBE):
        @pl.loop(0, span, step=8)
        def _(r):
            r = pl.multiple_of(r, 8)
            picked = []
            for j in range(8):
                p = partner_ref[i * span + r + j]
                picked.append(mated[lax.div(p, span), pl.ds(lax.rem(p, span), 1), :])
            out_ref[i, pl.ds(r, 8), :] = tile[i, pl.ds(r, 8), :] + jnp.concatenate(picked, axis=0)
    for q in range(QUARTERS):
        mate(q).wait_send()
    for t in range(steps):
        for slot in SOURCE:
            remote(slot, t).wait_send()


def shards(amplitudes, integrals, live_rows, partner):
    height, length = amplitudes.shape
    wide = integrals.shape[0]
    count = lax.axis_size("blk")
    repeats = count // CUBE
    if repeats > 1:
        groups = [[i + CUBE * j for j in range(repeats)] for i in range(CUBE)]
        amplitudes = lax.all_gather(amplitudes, "blk", axis=0, axis_index_groups=groups, tiled=True)
        live_rows = live_rows.reshape(repeats, CUBE).T.reshape(-1)
        block = partner // height
        partner = ((block % CUBE) * repeats + block // CUBE) * height + partner % height
        partner = partner.reshape(repeats, CUBE, height).transpose(1, 0, 2).reshape(-1)
    span = height * repeats
    rows = span // QUARTERS
    steps = QUARTERS * PIECES
    out = pl.pallas_call(
        functools.partial(kernel, height, length // PIECES),
        out_shape=jax.ShapeDtypeStruct((CUBE, span, wide), jnp.float32),
        in_specs=[
            pl.BlockSpec(memory_space=pltpu.SMEM),
            pl.BlockSpec(memory_space=pltpu.SMEM),
            pl.BlockSpec(memory_space=pl.ANY),
            pl.BlockSpec(memory_space=pl.ANY),
        ],
        out_specs=pl.BlockSpec(memory_space=pltpu.VMEM),
        scratch_shapes=[
            pltpu.VMEM((QUARTERS, CUBE, rows, length), jnp.bfloat16),
            pltpu.VMEM((wide, length), jnp.bfloat16),
            pltpu.VMEM((CUBE, span, wide), jnp.float32),
            pltpu.VMEM((CUBE, span, wide), jnp.float32),
            pltpu.SemaphoreType.DMA((CUBE, steps)),
            pltpu.SemaphoreType.DMA((CUBE, steps)),
            pltpu.SemaphoreType.DMA((QUARTERS,)),
            pltpu.SemaphoreType.DMA((PIECES,)),
            pltpu.SemaphoreType.DMA((QUARTERS,)),
            pltpu.SemaphoreType.DMA((QUARTERS,)),
        ],
        compiler_params=pltpu.CompilerParams(
            collective_id=0, has_side_effects=True, vmem_limit_bytes=56 * 1024 * 1024
        ),
    )(live_rows, partner, amplitudes, integrals)
    if repeats > 1:
        out = out.reshape(CUBE, repeats, height, wide).transpose(1, 0, 2, 3)
    return out.reshape(count * height, wide)


def solution(mesh):
    return jax.shard_map(
        shards,
        mesh=mesh,
        in_specs=(P("blk", None), P(("blk", "ab"), None), P(), P()),
        out_specs=P(None, ("blk", "ab")),
        check_vma=False,
    )
```

```python
import functools

import jax
import jax.numpy as jnp
from jax import lax
from jax.experimental import pallas as pl
from jax.experimental.pallas import tpu as pltpu
from jax.sharding import PartitionSpec as P

CUBE = 8
QUARTERS = 4
PIECES = 4
DIRECT = 2
SWAPPED = 1
WINDOW = 8
TURN = 6
LAG_RELAY = 3
LAG_DOT = 4

OWN, TWIN, FIRST, SECOND, ACROSS, TWIN_FIRST, TWIN_SECOND, TWIN_ACROSS = range(CUBE)


def kernel(
    height, depth, live_ref, partner_ref, a_ref, b_ref, out_ref,
    held, integrals, tile, mated,
    send_sem, recv_sem, own_sem, b_sem, mate_send, mate_recv,
):
    blk, ab = lax.axis_index("blk"), lax.axis_index("ab")
    ab_size = lax.axis_size("ab")
    b = lax.rem(blk, CUBE)
    base = blk - b
    core, x, y = lax.rem(b, 2), lax.rem(lax.div(b, 2), 2), lax.rem(lax.div(b, 4), 2)
    parity = lax.rem(ab, 2)
    flip = 1 - 2 * core
    near_x, near_y = b + 2 - 4 * x, b + 4 - 8 * y
    first = near_x + parity * (near_y - near_x)
    other = near_x + near_y - first
    diagonal = near_x + near_y - b
    blocks = [b, b + flip, first, diagonal, other, first + flip, diagonal + flip, other + flip]
    pairs = [i - core for i in (b, first, diagonal, other)]
    to_first = (base + first, ab)
    to_second = (base + other, ab)
    to_across = (blk, ab + 1 - 2 * parity)
    to_twin = (blk + flip, ab)
    to_mate = (blk, lax.rem(ab + ab_size // 2, ab_size))

    span = a_ref.shape[0]
    rows = span // QUARTERS
    repeats = span // height
    steps = QUARTERS * PIECES
    direct = range(steps - DIRECT, steps)
    swapped = range(steps - SWAPPED, steps)

    def route(slot, t):
        if slot == TWIN:
            return OWN, to_twin
        if slot == FIRST:
            return OWN, to_first
        if slot == SECOND:
            return (ACROSS, to_first) if t in swapped else (FIRST, to_second)
        if slot == ACROSS:
            return (OWN, to_second) if t in direct else (FIRST, to_across)
        return slot - 3, to_twin

    def remote(slot, t):
        q, columns = t // PIECES, pl.ds((t % PIECES) * depth, depth)
        origin, device = route(slot, t)
        if origin == OWN:
            src = a_ref.at[pl.ds(q * rows, rows), columns]
        else:
            src = held.at[q, origin, :, columns]
        return pltpu.make_async_remote_copy(
            src_ref=src,
            dst_ref=held.at[q, slot, :, columns],
            send_sem=send_sem.at[slot, t],
            recv_sem=recv_sem.at[slot, t],
            device_id=device,
            device_id_type=pl.DeviceIdType.MESH,
        )

    def mate(pair, q):
        if pair == 0:
            index, band = 0, pl.ds(0, span)
        else:
            index, band = 1 + q * 3 + pair - 1, pl.ds(q * rows, rows)
        where = (pl.ds(pairs[pair], 2), band, slice(None))
        return pltpu.make_async_remote_copy(
            src_ref=tile.at[where],
            dst_ref=mated.at[where],
            send_sem=mate_send.at[index],
            recv_sem=mate_recv.at[index],
            device_id=to_mate,
            device_id_type=pl.DeviceIdType.MESH,
        )

    mates = [(0, 0)] + [(pair, q) for q in range(QUARTERS) for pair in (1, 2, 3)]

    def load_b(k):
        columns = pl.ds(k * depth, depth)
        return pltpu.make_async_copy(b_ref.at[:, columns], integrals.at[:, columns], b_sem.at[k])

    def load_own(q):
        return pltpu.make_async_copy(a_ref.at[pl.ds(q * rows, rows), :], held.at[q, OWN], own_sem.at[q])

    def times(left, k):
        return lax.dot_general(
            left, integrals[:, pl.ds(k * depth, depth)], (((1,), (1,)), ((), ())),
            preferred_element_type=jnp.float32,
        )

    def keep(slot, q, part):
        group, inside = (q * rows) // height, (q * rows) % height
        row = inside + lax.broadcasted_iota(jnp.int32, part.shape, 0)
        limit = live_ref[blocks[slot] * repeats + group]
        tile[blocks[slot], pl.ds(q * rows, rows), :] = jnp.where(row < limit, part, 0.0)

    for q in range(QUARTERS):
        load_own(q).start()
    for k in range(PIECES):
        load_b(k).start()

    barrier = pltpu.get_barrier_semaphore()
    neighbours = (to_first, to_second, to_across, to_twin, to_mate)
    for device in neighbours:
        pl.semaphore_signal(barrier, inc=1, device_id=device, device_id_type=pl.DeviceIdType.MESH)
    pl.semaphore_wait(barrier, len(neighbours))

    for t in range(WINDOW):
        remote(FIRST, t).start()
    for t in direct:
        remote(ACROSS, t).start()
    for k in range(PIECES):
        for q in range(QUARTERS):
            remote(TWIN, q * PIECES + k).start()

    early, total = None, None
    for step in range(steps + LAG_DOT):
        if step < steps:
            remote(FIRST, step).wait_recv()
            if step not in swapped:
                remote(SECOND, step).start()
            if step not in direct:
                remote(ACROSS, step).start()
            remote(TWIN_FIRST, step).start()
            if step + WINDOW < steps:
                remote(FIRST, step + WINDOW).start()
        if step == TURN:
            for t in direct:
                remote(ACROSS, t).wait_recv()
                if t in swapped:
                    remote(SECOND, t).start()
                remote(TWIN_ACROSS, t).start()
        t = step - LAG_RELAY
        if 0 <= t < steps:
            remote(SECOND, t).wait_recv()
            remote(TWIN_SECOND, t).start()
            if t not in direct:
                remote(ACROSS, t).wait_recv()
                remote(TWIN_ACROSS, t).start()
        k = step - 1
        if 0 <= k < PIECES:
            load_b(k).wait()
            for q in range(QUARTERS):
                if k == 0:
                    load_own(q).wait()
                remote(TWIN, q * PIECES + k).wait_recv()
            left = held[:, OWN:FIRST, :, pl.ds(k * depth, depth)].reshape(2 * span, depth)
            early = times(left, k) if k == 0 else early + times(left, k)
            if k == PIECES - 1:
                for q in range(QUARTERS):
                    for slot in (OWN, TWIN):
                        start = (2 * q + slot) * rows
                        keep(slot, q, early[start:start + rows])
                mate(0, 0).start()
        t = step - LAG_DOT
        if t >= 0:
            q, k = t // PIECES, t % PIECES
            for slot in (TWIN_FIRST, TWIN_SECOND, TWIN_ACROSS):
                remote(slot, t).wait_recv()
            left = held[q, FIRST:, :, pl.ds(k * depth, depth)].reshape((CUBE - 2) * rows, depth)
            total = times(left, k) if k == 0 else total + times(left, k)
            if k == PIECES - 1:
                for slot in range(FIRST, CUBE):
                    start = (slot - FIRST) * rows
                    keep(slot, q, total[start:start + rows])
                for pair in (1, 2, 3):
                    mate(pair, q).start()

    for pair, q in mates:
        mate(pair, q).wait_recv()
    for i in range(CUBE):
        @pl.loop(0, span, step=8)
        def _(r):
            r = pl.multiple_of(r, 8)
            picked = []
            for j in range(8):
                p = partner_ref[i * span + r + j]
                picked.append(mated[lax.div(p, span), pl.ds(lax.rem(p, span), 1), :])
            out_ref[i, pl.ds(r, 8), :] = tile[i, pl.ds(r, 8), :] + jnp.concatenate(picked, axis=0)
    for pair, q in mates:
        mate(pair, q).wait_send()
    for t in range(steps):
        for slot in range(TWIN, CUBE):
            remote(slot, t).wait_send()


def shards(amplitudes, integrals, live_rows, partner):
    height, length = amplitudes.shape
    wide = integrals.shape[0]
    count = lax.axis_size("blk")
    repeats = count // CUBE
    if repeats > 1:
        groups = [[i + CUBE * j for j in range(repeats)] for i in range(CUBE)]
        amplitudes = lax.all_gather(amplitudes, "blk", axis=0, axis_index_groups=groups, tiled=True)
        live_rows = live_rows.reshape(repeats, CUBE).T.reshape(-1)
        block = partner // height
        partner = ((block % CUBE) * repeats + block // CUBE) * height + partner % height
        partner = partner.reshape(repeats, CUBE, height).transpose(1, 0, 2).reshape(-1)
    span = height * repeats
    rows = span // QUARTERS
    steps = QUARTERS * PIECES
    out = pl.pallas_call(
        functools.partial(kernel, height, length // PIECES),
        out_shape=jax.ShapeDtypeStruct((CUBE, span, wide), jnp.float32),
        in_specs=[
            pl.BlockSpec(memory_space=pltpu.SMEM),
            pl.BlockSpec(memory_space=pltpu.SMEM),
            pl.BlockSpec(memory_space=pl.ANY),
            pl.BlockSpec(memory_space=pl.ANY),
        ],
        out_specs=pl.BlockSpec(memory_space=pltpu.VMEM),
        scratch_shapes=[
            pltpu.VMEM((QUARTERS, CUBE, rows, length), jnp.bfloat16),
            pltpu.VMEM((wide, length), jnp.bfloat16),
            pltpu.VMEM((CUBE, span, wide), jnp.float32),
            pltpu.VMEM((CUBE, span, wide), jnp.float32),
            pltpu.SemaphoreType.DMA((CUBE, steps)),
            pltpu.SemaphoreType.DMA((CUBE, steps)),
            pltpu.SemaphoreType.DMA((QUARTERS,)),
            pltpu.SemaphoreType.DMA((PIECES,)),
            pltpu.SemaphoreType.DMA((1 + 3 * QUARTERS,)),
            pltpu.SemaphoreType.DMA((1 + 3 * QUARTERS,)),
        ],
        compiler_params=pltpu.CompilerParams(
            collective_id=0, has_side_effects=True, vmem_limit_bytes=56 * 1024 * 1024
        ),
    )(live_rows, partner, amplitudes, integrals)
    if repeats > 1:
        out = out.reshape(CUBE, repeats, height, wide).transpose(1, 0, 2, 3)
    return out.reshape(count * height, wide)


def solution(mesh):
    return jax.shard_map(
        shards,
        mesh=mesh,
        in_specs=(P("blk", None), P(("blk", "ab"), None), P(), P()),
        out_specs=P(None, ("blk", "ab")),
        check_vma=False,
    )
```

```python
import functools

import jax
import jax.numpy as jnp
from jax import lax
from jax.experimental import pallas as pl
from jax.experimental.pallas import tpu as pltpu
from jax.sharding import PartitionSpec as P

CUBE = 8
QUARTERS = 4
PIECES = 4
DIRECT = 2
SWAPPED = 1
WINDOW = 8
TURN = 6
LAG_RELAY = 4
LAG_DOT = 6

OWN, TWIN, FIRST, SECOND, ACROSS, TWIN_FIRST, TWIN_SECOND, TWIN_ACROSS = range(CUBE)


def kernel(
    height, depth, live_ref, partner_ref, a_ref, b_ref, out_ref,
    held, integrals, tile, mated,
    send_sem, recv_sem, own_sem, b_sem, mate_send, mate_recv,
):
    blk, ab = lax.axis_index("blk"), lax.axis_index("ab")
    ab_size = lax.axis_size("ab")
    b = lax.rem(blk, CUBE)
    base = blk - b
    core, x, y = lax.rem(b, 2), lax.rem(lax.div(b, 2), 2), lax.rem(lax.div(b, 4), 2)
    parity = lax.rem(ab, 2)
    flip = 1 - 2 * core
    near_x, near_y = b + 2 - 4 * x, b + 4 - 8 * y
    first = near_x + parity * (near_y - near_x)
    other = near_x + near_y - first
    diagonal = near_x + near_y - b
    blocks = [b, b + flip, first, diagonal, other, first + flip, diagonal + flip, other + flip]
    pairs = [i - core for i in (b, first, diagonal, other)]
    to_first = (base + first, ab)
    to_second = (base + other, ab)
    to_across = (blk, ab + 1 - 2 * parity)
    to_twin = (blk + flip, ab)
    to_mate = (blk, lax.rem(ab + ab_size // 2, ab_size))

    span = a_ref.shape[0]
    rows = span // QUARTERS
    repeats = span // height
    steps = QUARTERS * PIECES
    direct = range(steps - DIRECT, steps)
    swapped = range(steps - SWAPPED, steps)

    def route(slot, t):
        if slot == TWIN:
            return OWN, to_twin
        if slot == FIRST:
            return OWN, to_first
        if slot == SECOND:
            return (ACROSS, to_first) if t in swapped else (FIRST, to_second)
        if slot == ACROSS:
            return (OWN, to_second) if t in direct else (FIRST, to_across)
        return slot - 3, to_twin

    def remote(slot, t):
        q, columns = t // PIECES, pl.ds((t % PIECES) * depth, depth)
        origin, device = route(slot, t)
        if origin == OWN:
            src = a_ref.at[pl.ds(q * rows, rows), columns]
        else:
            src = held.at[q, origin, :, columns]
        return pltpu.make_async_remote_copy(
            src_ref=src,
            dst_ref=held.at[q, slot, :, columns],
            send_sem=send_sem.at[slot, t],
            recv_sem=recv_sem.at[slot, t],
            device_id=device,
            device_id_type=pl.DeviceIdType.MESH,
        )

    def mate(pair, q):
        if pair == 0:
            index, band = 0, pl.ds(0, span)
        else:
            index, band = 1 + q * 3 + pair - 1, pl.ds(q * rows, rows)
        where = (pl.ds(pairs[pair], 2), band, slice(None))
        return pltpu.make_async_remote_copy(
            src_ref=tile.at[where],
            dst_ref=mated.at[where],
            send_sem=mate_send.at[index],
            recv_sem=mate_recv.at[index],
            device_id=to_mate,
            device_id_type=pl.DeviceIdType.MESH,
        )

    mates = [(0, 0)] + [(pair, q) for q in range(QUARTERS) for pair in (1, 2, 3)]

    def load_b(k):
        columns = pl.ds(k * depth, depth)
        return pltpu.make_async_copy(b_ref.at[:, columns], integrals.at[:, columns], b_sem.at[k])

    def load_own(q):
        return pltpu.make_async_copy(a_ref.at[pl.ds(q * rows, rows), :], held.at[q, OWN], own_sem.at[q])

    def times(left, k):
        return lax.dot_general(
            left, integrals[:, pl.ds(k * depth, depth)], (((1,), (1,)), ((), ())),
            preferred_element_type=jnp.float32,
        )

    def keep(slot, q, part):
        group, inside = (q * rows) // height, (q * rows) % height
        row = inside + lax.broadcasted_iota(jnp.int32, part.shape, 0)
        limit = live_ref[blocks[slot] * repeats + group]
        tile[blocks[slot], pl.ds(q * rows, rows), :] = jnp.where(row < limit, part, 0.0)

    for q in range(QUARTERS):
        load_own(q).start()
    for k in range(PIECES):
        load_b(k).start()

    barrier = pltpu.get_barrier_semaphore()
    neighbours = (to_first, to_second, to_across, to_twin, to_mate)
    for device in neighbours:
        pl.semaphore_signal(barrier, inc=1, device_id=device, device_id_type=pl.DeviceIdType.MESH)
    pl.semaphore_wait(barrier, len(neighbours))

    for t in range(WINDOW):
        remote(FIRST, t).start()
    for t in direct:
        remote(ACROSS, t).start()
    for k in range(PIECES):
        for q in range(QUARTERS):
            remote(TWIN, q * PIECES + k).start()

    early, total = None, None
    for step in range(steps + LAG_DOT):
        if step < steps:
            remote(FIRST, step).wait_recv()
            if step not in swapped:
                remote(SECOND, step).start()
            if step not in direct:
                remote(ACROSS, step).start()
            remote(TWIN_FIRST, step).start()
            if step + WINDOW < steps:
                remote(FIRST, step + WINDOW).start()
        if step == TURN:
            for t in direct:
                remote(ACROSS, t).wait_recv()
                if t in swapped:
                    remote(SECOND, t).start()
                remote(TWIN_ACROSS, t).start()
        t = step - LAG_RELAY
        if 0 <= t < steps:
            remote(SECOND, t).wait_recv()
            remote(TWIN_SECOND, t).start()
            if t not in direct:
                remote(ACROSS, t).wait_recv()
                remote(TWIN_ACROSS, t).start()
        k = step - 1
        if 0 <= k < PIECES:
            load_b(k).wait()
            for q in range(QUARTERS):
                if k == 0:
                    load_own(q).wait()
                remote(TWIN, q * PIECES + k).wait_recv()
            left = held[:, OWN:FIRST, :, pl.ds(k * depth, depth)].reshape(2 * span, depth)
            early = times(left, k) if k == 0 else early + times(left, k)
            if k == PIECES - 1:
                for q in range(QUARTERS):
                    for slot in (OWN, TWIN):
                        start = (2 * q + slot) * rows
                        keep(slot, q, early[start:start + rows])
                mate(0, 0).start()
        t = step - LAG_DOT
        if t >= 0:
            q, k = t // PIECES, t % PIECES
            for slot in (TWIN_FIRST, TWIN_SECOND, TWIN_ACROSS):
                remote(slot, t).wait_recv()
            left = held[q, FIRST:, :, pl.ds(k * depth, depth)].reshape((CUBE - 2) * rows, depth)
            total = times(left, k) if k == 0 else total + times(left, k)
            if k == PIECES - 1:
                for slot in range(FIRST, CUBE):
                    start = (slot - FIRST) * rows
                    keep(slot, q, total[start:start + rows])
                for pair in (1, 2, 3):
                    mate(pair, q).start()

    for pair, q in mates:
        mate(pair, q).wait_recv()
    for i in range(CUBE):
        @pl.loop(0, span, step=8)
        def _(r):
            r = pl.multiple_of(r, 8)
            picked = []
            for j in range(8):
                p = partner_ref[i * span + r + j]
                picked.append(mated[lax.div(p, span), pl.ds(lax.rem(p, span), 1), :])
            out_ref[i, pl.ds(r, 8), :] = tile[i, pl.ds(r, 8), :] + jnp.concatenate(picked, axis=0)
    for pair, q in mates:
        mate(pair, q).wait_send()
    for t in range(steps):
        for slot in range(TWIN, CUBE):
            remote(slot, t).wait_send()


def shards(amplitudes, integrals, live_rows, partner):
    height, length = amplitudes.shape
    wide = integrals.shape[0]
    count = lax.axis_size("blk")
    repeats = count // CUBE
    if repeats > 1:
        groups = [[i + CUBE * j for j in range(repeats)] for i in range(CUBE)]
        amplitudes = lax.all_gather(amplitudes, "blk", axis=0, axis_index_groups=groups, tiled=True)
        live_rows = live_rows.reshape(repeats, CUBE).T.reshape(-1)
        block = partner // height
        partner = ((block % CUBE) * repeats + block // CUBE) * height + partner % height
        partner = partner.reshape(repeats, CUBE, height).transpose(1, 0, 2).reshape(-1)
    span = height * repeats
    rows = span // QUARTERS
    steps = QUARTERS * PIECES
    out = pl.pallas_call(
        functools.partial(kernel, height, length // PIECES),
        out_shape=jax.ShapeDtypeStruct((CUBE, span, wide), jnp.float32),
        in_specs=[
            pl.BlockSpec(memory_space=pltpu.SMEM),
            pl.BlockSpec(memory_space=pltpu.SMEM),
            pl.BlockSpec(memory_space=pl.ANY),
            pl.BlockSpec(memory_space=pl.ANY),
        ],
        out_specs=pl.BlockSpec(memory_space=pltpu.VMEM),
        scratch_shapes=[
            pltpu.VMEM((QUARTERS, CUBE, rows, length), jnp.bfloat16),
            pltpu.VMEM((wide, length), jnp.bfloat16),
            pltpu.VMEM((CUBE, span, wide), jnp.float32),
            pltpu.VMEM((CUBE, span, wide), jnp.float32),
            pltpu.SemaphoreType.DMA((CUBE, steps)),
            pltpu.SemaphoreType.DMA((CUBE, steps)),
            pltpu.SemaphoreType.DMA((QUARTERS,)),
            pltpu.SemaphoreType.DMA((PIECES,)),
            pltpu.SemaphoreType.DMA((1 + 3 * QUARTERS,)),
            pltpu.SemaphoreType.DMA((1 + 3 * QUARTERS,)),
        ],
        compiler_params=pltpu.CompilerParams(
            collective_id=0, has_side_effects=True, vmem_limit_bytes=56 * 1024 * 1024
        ),
    )(live_rows, partner, amplitudes, integrals)
    if repeats > 1:
        out = out.reshape(CUBE, repeats, height, wide).transpose(1, 0, 2, 3)
    return out.reshape(count * height, wide)


def solution(mesh):
    return jax.shard_map(
        shards,
        mesh=mesh,
        in_specs=(P("blk", None), P(("blk", "ab"), None), P(), P()),
        out_specs=P(None, ("blk", "ab")),
        check_vma=False,
    )
```
